512 devices in a mesh: subtree: 16 (over z), forest: 32 (over y, x, core).
Axes of the slice: x: 4, y: 4, z: 16, core: 2. Of those that a mesh axis runs over, the one named last changes fastest.
Arguments:
- panels: bfloat16 [16, 32, 1024, 2048], P('subtree', 'forest'), may hold values from -0.75 to 0.75
- pattern: int32 [16, 32, 8, 8], P('subtree', 'forest'), may hold values from 0 to 1, as said below
- child_map: int32 [16, 32, 8], P('subtree', 'forest'), may hold values from 0 to 7, each once within a row
- ancestor_map: int32 [16, 32, 8], P('subtree', 'forest'), may hold values from 0 to 95, as said below
Outputs:
- ancestors: float32 [16, 96, 64, 128], P('subtree', 'forest')
The draws below stay inside these ranges and needn't reach their ends.
Inputs may be any that keep to these rules, and one draw needn't show every extreme that they name: pattern[s, f, i, j] = pattern[s, f, i, i] * pattern[s, f, j, j], so each pattern is symmetric; every panel has at least one occupied and at least one empty block row. No two entries of ancestor_map[s, f, :] have the same value of entry // 3.
All inputs are finite; a program needn't handle non-finite values.
Results may differ from the reference program's by a relative error of at most 0.0003.
Values sent between devices are 32-bit elements; how exact they have to be, the bound alone decides.
A program may use at most 64 MiB of HBM per device.

```python
import jax
import jax.numpy as jnp
from jax import lax

K = 2048
BLOCK = 128
NB = 8
ANC_DEV = 3
SUBS = 16
TREES = 32
R = 1024
PIECE = 64
ANC = 96


def draw_pattern(key, part):
    count = SUBS * TREES
    occupied = (jax.random.randint(jax.random.fold_in(key, 41), (count, NB), 0, 100) < 63).astype(jnp.int32)
    pick = jax.random.randint(jax.random.fold_in(key, 43), (count, 1), 0, NB)
    column = jnp.arange(NB, dtype=jnp.int32)[None, :]
    occupied = jnp.where(column == pick, 1, jnp.where(column == (pick + 1) % NB, 0, occupied)).astype(jnp.int32)
    pattern_all = occupied[:, :, None] * occupied[:, None, :]
    return pattern_all.reshape(SUBS, TREES, NB, NB).astype(jnp.int32)


def draw_ancestor_map(key, part):
    count = SUBS * TREES
    keys = jax.random.split(jax.random.fold_in(key, 17), count)
    owners = jax.vmap(lambda one_key: jax.random.permutation(one_key, TREES)[:NB])(keys)
    slots = jax.random.randint(jax.random.fold_in(key, 29), (count, NB), 0, ANC_DEV)
    first_owner = jnp.concatenate([jnp.zeros((1,), jnp.int32), jnp.arange(TREES - NB + 1, TREES, dtype=jnp.int32)])
    first_slot = jnp.concatenate([jnp.zeros((NB - 1,), jnp.int32), jnp.full((1,), ANC_DEV - 1, jnp.int32)])
    device_rank = jnp.arange(count, dtype=jnp.int32)[:, None]
    owners = jnp.where(device_rank == 0, first_owner[None, :], owners.astype(jnp.int32))
    slots = jnp.where(device_rank == 0, first_slot[None, :], slots.astype(jnp.int32))
    return (owners * ANC_DEV + slots).reshape(SUBS, TREES, NB).astype(jnp.int32)


def block_levels(key, shape, shards, smallest, high):
    def one(position, blocks):
        draws = jax.random.uniform(jax.random.fold_in(jax.random.fold_in(key, 6), position), (blocks,), jnp.float32, smallest / len(shards), high / len(shards))
        return jnp.repeat(jnp.exp(draws), shape[position] // blocks).reshape((-1,) + (1,) * (len(shape) - position - 1))

    level = one(*shards[0])
    for cut in shards[1:]:
        level = level * one(*cut)
    return level


def gaussian(own_key, dims, scale, bound, cuts=(), kind=jnp.bfloat16):
    array = jax.random.normal(own_key, dims, jnp.float32) * scale
    if len(cuts) > 0:
        array = block_levels(own_key, dims, cuts, -0.22, 0.18) * array
    return jnp.clip(array, min=-bound, max=bound).astype(kind)


def setup_inputs(seed: int = 0) -> dict:
    streams_of = jax.random.split(jax.random.key(seed), 5)
    return {
        "panels": gaussian(streams_of[0], (SUBS, TREES, R, K), 0.125, 0.75, ((0, 16), (1, 32))),
        "pattern": draw_pattern(jax.random.fold_in(streams_of[4], 71), 0),
        "child_map": jax.vmap(lambda own: jax.random.permutation(own, NB))(jax.random.split(streams_of[2], SUBS * TREES)).reshape((SUBS, TREES, NB)).astype(jnp.int32),
        "ancestor_map": draw_ancestor_map(jax.random.fold_in(streams_of[4], 71), 0),
    }


def contribution(panel_one, pattern_one, map_one):
    blocks = panel_one.reshape(NB, BLOCK, K).astype(jnp.float32)
    one_hot = (map_one[:, None] == jnp.arange(NB, dtype=jnp.int32)[None, :]).astype(jnp.float32)
    reordered = jnp.einsum("im,ipk->mpk", one_hot, blocks, precision=lax.Precision.HIGHEST).astype(jnp.bfloat16)
    flat_rows = reordered.reshape(R, K)
    moved_pattern = jnp.dot(jnp.dot(one_hot.T, pattern_one.astype(jnp.float32), precision=lax.Precision.HIGHEST), one_hot, precision=lax.Precision.HIGHEST)
    update = jnp.dot(flat_rows, flat_rows.T, preferred_element_type=jnp.float32)
    return (update.reshape(NB, BLOCK, NB, BLOCK) * moved_pattern[:, None, :, None]).reshape(R, R)


def reference(panels, pattern, child_map, ancestor_map):
    def forest_total(forest_index):
        def accumulate(running, sub_index):
            term = contribution(panels[sub_index, forest_index], pattern[sub_index, forest_index], child_map[sub_index, forest_index])
            return running + term, None
        running, unused = lax.scan(accumulate, jnp.zeros((R, R), jnp.float32), jnp.arange(SUBS, dtype=jnp.int32))
        return running

    parent = lax.map(forest_total, jnp.arange(TREES, dtype=jnp.int32))
    pieces = parent.reshape(TREES, SUBS, PIECE, NB, BLOCK).transpose(1, 0, 3, 2, 4)
    slot_hot = (ancestor_map[..., None] == jnp.arange(ANC, dtype=jnp.int32)).astype(jnp.float32)
    return jnp.einsum("sfca,sfcpq->sapq", slot_hot, pieces, precision=lax.Precision.HIGHEST)
```

```python
import jax
import jax.numpy as jnp
from jax import lax
from jax.experimental import pallas as pl
from jax.experimental.pallas import tpu as pltpu
from jax.sharding import PartitionSpec as P

MESH = pl.DeviceIdType.MESH
ANC_DEV = 3
OWNED = (5, 2, 1, 4, 0)
SENT = 3
LAG = (0, 0, 0, 0, 0)


def kernel(
    subs, trees,
    child_ref, pattern_ref, anc_ref, panel_ref, out_ref,
    rows, gram, recv_l, recv_s, piece, x_send, x_recv, w_send, w_recv, t_send, t_recv,
    l_out, l_in, s_out, s_in, x_out, x_in, w_out, w_in, t_out, t_in,
):
    nb = child_ref.shape[0]
    block = panel_ref.shape[1]
    part = block // 2
    half = subs // 2
    s = lax.axis_index("subtree")
    f = lax.axis_index("forest")
    m = s // 2
    side = s % 2
    sigma = 1 - 2 * (f % 2)

    def z(offset):
        return (s + offset + 4 * subs) % subs

    def block_row(offset):
        return (m + offset + 4 * nb) % nb

    barrier = pltpu.get_barrier_semaphore()
    others = [(z(0) // 2 * 2 + 1 - side, f)]
    for e in (1, 2, 3):
        for sign in (1, -1):
            for j in (0, 1):
                others.append((2 * block_row(sign * e) + j, f))
    for other in others:
        pl.semaphore_signal(barrier, inc=1, device_id=other, device_id_type=MESH)

    @pl.loop(1, trees)
    def _(r):
        pl.semaphore_signal(
            barrier, inc=1, device_id=(s, (f + r) % trees), device_id_type=MESH
        )

    @pl.loop(0, nb)
    def _(to):
        source = jnp.int32(0)
        for i in range(nb):
            source = jnp.where(child_ref[i] == to, i, source)
        keep = jnp.int32(0)
        for i in range(nb):
            keep = jnp.where(child_ref[i] == to, pattern_ref[i, i], keep)
        chunk = panel_ref[source]
        rows[pl.ds(pl.multiple_of(to * block, block), block), :] = chunk * keep.astype(
            jnp.float32
        ).astype(jnp.bfloat16)

    @pl.loop(0, nb // 2)
    def _(u):
        at = pl.ds(pl.multiple_of(u * 2 * block, 2 * block), 2 * block)
        product = lax.dot_general(
            rows[at, :], rows[...], (((1,), (1,)), ((), ())), preferred_element_type=jnp.float32
        )
        for n in range(nb):
            gram[n, at, :] = product[:, n * block : (n + 1) * block]

    pl.semaphore_wait(barrier, len(others) + trees - 1)

    row = lax.broadcasted_iota(jnp.int32, w_send.shape[1:], 0)

    def weights(owner):
        total = jnp.zeros(row.shape, jnp.float32)
        for c in range(nb):
            total += jnp.where(row == anc_ref[c] - ANC_DEV * owner, 1.0, 0.0)
        return total

    def w_copy(r, owner, source):
        return pltpu.make_async_remote_copy(
            src_ref=w_send.at[owner], dst_ref=w_recv.at[source],
            send_sem=w_out.at[r], recv_sem=w_in.at[r],
            device_id=(s, owner), device_id_type=MESH,
        )

    def t_copy(r, owner, source):
        return pltpu.make_async_remote_copy(
            src_ref=t_send.at[owner], dst_ref=t_recv.at[source],
            send_sem=t_out.at[r], recv_sem=t_in.at[r],
            device_id=(s, owner), device_id_type=MESH,
        )

    def own(target, j):
        return gram.at[
            block_row_of(target, j), pl.ds(pl.multiple_of(target * part, part), part), :
        ]

    def block_row_of(target, j):
        return (target // 2 + OWNED[j]) % nb

    def chain(k, j, buffers, outs, ins, direction, steps):
        target = z(direction * (steps - k))
        if k == 0:
            source = own(target, j)
        else:
            source = buffers.at[k - 1, j]
        return pltpu.make_async_remote_copy(
            src_ref=source, dst_ref=buffers.at[k, j],
            send_sem=outs.at[k, j], recv_sem=ins.at[k, j],
            device_id=(z(direction), f), device_id_type=MESH,
        )

    def advance(k, j, buffers, outs, ins, direction, steps):
        if k > 0:
            chain(k - 1, j, buffers, outs, ins, direction, steps).wait_recv()
            buffers[k - 1, j] = buffers[k - 1, j] + own(z(direction * (steps - k)), j)[...]
        chain(k, j, buffers, outs, ins, direction, steps).start()

    long_chain = (recv_l, l_out, l_in, sigma, half)
    short_chain = (recv_s, s_out, s_in, -sigma, half - 1)

    def x_copy(j, other):
        n = block_row(OWNED[j])
        return pltpu.make_async_remote_copy(
            src_ref=x_send.at[j, other], dst_ref=x_recv.at[j, side],
            send_sem=x_out.at[j, other], recv_sem=x_in.at[j, side],
            device_id=(2 * n + other, f), device_id_type=MESH,
        )

    def x_arrival(j, other):
        return pltpu.make_async_remote_copy(
            src_ref=x_send.at[j, other], dst_ref=x_recv.at[j, other],
            send_sem=x_out.at[j, other], recv_sem=x_in.at[j, other],
            device_id=(2 * block_row(OWNED[j]) + other, f), device_id_type=MESH,
        )

    quarter = part // 2

    def finish(j):
        chain(half - 1, j, *long_chain).wait_recv()
        chain(half - 2, j, *short_chain).wait_recv()
        tile = own(z(0), j)[...] + (recv_l[half - 1, j] + recv_s[half - 2, j])
        piece[block_row(OWNED[j])] = tile
        if j < SENT:
            stacked = jnp.concatenate([tile, pltpu.roll(tile, block - quarter, 1)], axis=0)
            turned = stacked.T
            for other in (0, 1):
                x_send[j, other] = turned[other * part : other * part + quarter, :]
                x_copy(j, other).start()

    order = sorted(
        (k + LAG[j], j, k) for k in range(half + 1) for j in range(len(OWNED))
    )
    started = False
    for _, j, k in order:
        if k < half:
            advance(k, j, *long_chain)
        if k < half - 1:
            advance(k, j, *short_chain)
        if k == half:
            finish(j)
        if k == 1 and not started:
            started = True
            w_send[f] = weights(f)
            w_recv[f] = weights(f)

            @pl.loop(1, trees)
            def _(r):
                owner = (f + r) % trees
                w_send[owner] = weights(owner)
                w_copy(r, owner, f).start()

    lane = lax.broadcasted_iota(jnp.int32, (quarter, block), 1)
    for j in range(SENT):
        for other in (0, 1):
            x_arrival(j, other).wait_recv()
        low = x_recv[j, 0]
        high = x_recv[j, 1]
        n = block_row(-OWNED[j])
        piece[n, :quarter, :] = jnp.where(lane < part, low, pltpu.roll(high, part, 1))
        piece[n, quarter:, :] = jnp.where(lane < part, pltpu.roll(low, part, 1), high)
    piece[nb] = jnp.zeros(piece.shape[1:], jnp.float32)

    def chosen(owner):
        index = jnp.int32(nb)
        for c in range(nb):
            first = anc_ref[c] - ANC_DEV * owner
            index = jnp.where((first >= 0) & (first < ANC_DEV), c, index)
        return piece[index]

    @pl.loop(1, trees)
    def _(r):
        owner = (f + r) % trees
        t_send[owner] = chosen(owner)
        t_copy(r, owner, f).start()

    def added(source, tile, totals):
        weight = w_recv[source]
        return tuple(totals[a] + weight[a : a + 1, :] * tile for a in range(ANC_DEV))

    zero = jnp.zeros(piece.shape[1:], jnp.float32)
    totals = added(f, chosen(f), (zero,) * ANC_DEV)

    def gather(r, totals):
        source = (f + trees - r) % trees
        w_copy(r, source, source).wait_recv()
        t_copy(r, source, source).wait_recv()
        return added(source, t_recv[source], totals)

    totals = lax.fori_loop(1, trees, gather, totals)
    for a in range(ANC_DEV):
        out_ref[a] = totals[a]

    for j in range(len(OWNED)):
        for k in range(half):
            chain(k, j, *long_chain).wait_send()
        for k in range(half - 1):
            chain(k, j, *short_chain).wait_send()
    for j in range(SENT):
        for other in (0, 1):
            x_copy(j, other).wait_send()

    @pl.loop(1, trees)
    def _(r):
        owner = (f + r) % trees
        w_copy(r, owner, f).wait_send()
        t_copy(r, owner, f).wait_send()


def solution(mesh):
    subs, trees = mesh.shape["subtree"], mesh.shape["forest"]

    def per_device(panels, pattern, child_map, ancestor_map):
        rows, depth = panels.shape[2:]
        nb = child_map.shape[2]
        block = rows // nb
        part = block // 2
        half = subs // 2
        owned = len(OWNED)
        dma = pltpu.SemaphoreType.DMA
        smem = pl.BlockSpec(memory_space=pltpu.SMEM)
        vmem = pl.BlockSpec(memory_space=pltpu.VMEM)
        f32 = jnp.float32
        out = pl.pallas_call(
            lambda *refs: kernel(subs, trees, *refs),
            name="assemble",
            out_shape=jax.ShapeDtypeStruct((ANC_DEV, part, block), f32),
            in_specs=[smem, smem, smem, vmem],
            out_specs=vmem,
            scratch_shapes=[
                pltpu.VMEM((rows, depth), jnp.bfloat16),
                pltpu.VMEM((nb, rows, block), f32),
                pltpu.VMEM((half, owned, part, block), f32),
                pltpu.VMEM((half - 1, owned, part, block), f32),
                pltpu.VMEM((nb + 1, part, block), f32),
                pltpu.VMEM((SENT, 2, part // 2, block), f32),
                pltpu.VMEM((SENT, 2, part // 2, block), f32),
                pltpu.VMEM((trees, 8, block), f32),
                pltpu.VMEM((trees, 8, block), f32),
                pltpu.VMEM((trees, part, block), f32),
                pltpu.VMEM((trees, part, block), f32),
                dma((half, owned)), dma((half, owned)),
                dma((half - 1, owned)), dma((half - 1, owned)),
                dma((SENT, 2)), dma((SENT, 2)),
                dma((trees,)), dma((trees,)),
                dma((trees,)), dma((trees,)),
            ],
            compiler_params=pltpu.CompilerParams(
                collective_id=0, has_side_effects=True, vmem_limit_bytes=60 * 2**20
            ),
        )(child_map[0, 0], pattern[0, 0], ancestor_map[0, 0], panels.reshape(nb, block, depth))
        return out[None]

    return jax.shard_map(
        per_device,
        mesh=mesh,
        in_specs=(
            P("subtree", "forest", None, None),
            P("subtree", "forest", None, None),
            P("subtree", "forest", None),
            P("subtree", "forest", None),
        ),
        out_specs=P("subtree", "forest", None, None),
        check_vma=False,
    )
```

```python
import jax
import jax.numpy as jnp
from jax import lax
from jax.experimental import pallas as pl
from jax.experimental.pallas import tpu as pltpu
from jax.sharding import PartitionSpec as P

MESH = pl.DeviceIdType.MESH
ANC_DEV = 3
OWNED = (5, 2, 1, 4, 0)
SENT = 3
LAG = (0, 0, 0, 0, 0)


def kernel(
    subs, trees,
    child_ref, pattern_ref, anc_ref, panel_hbm, out_ref,
    panel_ref, rows, gram, recv_l, recv_s, piece, x_send, x_recv, w_send, w_recv, t_send, t_recv,
    l_out, l_in, s_out, s_in, x_out, x_in, w_out, w_in, t_out, t_in, panel_in,
):
    nb = child_ref.shape[0]
    block = panel_hbm.shape[1]
    part = block // 2
    half = subs // 2
    s = lax.axis_index("subtree")
    f = lax.axis_index("forest")
    m = s // 2
    side = s % 2
    sigma = 1 - 2 * (f % 2)

    def z(offset):
        return (s + offset + 4 * subs) % subs

    def block_row(offset):
        return (m + offset + 4 * nb) % nb

    load = pltpu.make_async_copy(panel_hbm, panel_ref, panel_in)
    load.start()

    barrier = pltpu.get_barrier_semaphore()
    for step in (1, -1):
        pl.semaphore_signal(barrier, inc=1, device_id=(z(step), f), device_id_type=MESH)

    @pl.loop(1, trees)
    def _(r):
        pl.semaphore_signal(
            barrier, inc=1, device_id=(s, (f + r) % trees), device_id_type=MESH
        )

    load.wait()

    @pl.loop(0, nb)
    def _(to):
        source = jnp.int32(0)
        for i in range(nb):
            source = jnp.where(child_ref[i] == to, i, source)
        keep = jnp.int32(0)
        for i in range(nb):
            keep = jnp.where(child_ref[i] == to, pattern_ref[i, i], keep)
        chunk = panel_ref[source]
        rows[pl.ds(pl.multiple_of(to * block, block), block), :] = chunk * keep.astype(
            jnp.float32
        ).astype(jnp.bfloat16)

    def multiply(u):
        at = pl.ds(pl.multiple_of(u * 2 * block, 2 * block), 2 * block)
        product = lax.dot_general(
            rows[at, :], rows[...], (((1,), (1,)), ((), ())), preferred_element_type=jnp.float32
        )
        for n in range(nb):
            gram[n, at, :] = product[:, n * block : (n + 1) * block]

    groups = nb // 2
    group, place = s // 4, s % 4
    near = (place // 2) * 2 + 1
    group_order = [(group + g) % groups for g in (2, near, 4 - near, 0)]

    row = lax.broadcasted_iota(jnp.int32, w_send.shape[1:], 0)

    def weights(owner):
        total = jnp.zeros(row.shape, jnp.float32)
        for c in range(nb):
            total += jnp.where(row == anc_ref[c] - ANC_DEV * owner, 1.0, 0.0)
        return total

    def w_copy(r, owner, source):
        return pltpu.make_async_remote_copy(
            src_ref=w_send.at[owner], dst_ref=w_recv.at[source],
            send_sem=w_out.at[r], recv_sem=w_in.at[r],
            device_id=(s, owner), device_id_type=MESH,
        )

    def t_copy(r, owner, source):
        return pltpu.make_async_remote_copy(
            src_ref=t_send.at[owner], dst_ref=t_recv.at[source],
            send_sem=t_out.at[r], recv_sem=t_in.at[r],
            device_id=(s, owner), device_id_type=MESH,
        )

    def own(target, j):
        return gram.at[
            block_row_of(target, j), pl.ds(pl.multiple_of(target * part, part), part), :
        ]

    def block_row_of(target, j):
        return (target // 2 + OWNED[j]) % nb

    def chain(k, j, buffers, outs, ins, direction, steps):
        target = z(direction * (steps - k))
        if k == 0:
            source = own(target, j)
        else:
            source = buffers.at[k - 1, j]
        return pltpu.make_async_remote_copy(
            src_ref=source, dst_ref=buffers.at[k, j],
            send_sem=outs.at[k, j], recv_sem=ins.at[k, j],
            device_id=(z(direction), f), device_id_type=MESH,
        )

    def advance(k, j, buffers, outs, ins, direction, steps):
        if k > 0:
            chain(k - 1, j, buffers, outs, ins, direction, steps).wait_recv()
            buffers[k - 1, j] = buffers[k - 1, j] + own(z(direction * (steps - k)), j)[...]
        chain(k, j, buffers, outs, ins, direction, steps).start()

    long_chain = (recv_l, l_out, l_in, sigma, half)
    short_chain = (recv_s, s_out, s_in, -sigma, half - 1)

    def x_copy(j, other):
        n = block_row(OWNED[j])
        return pltpu.make_async_remote_copy(
            src_ref=x_send.at[j, other], dst_ref=x_recv.at[j, side],
            send_sem=x_out.at[j, other], recv_sem=x_in.at[j, side],
            device_id=(2 * n + other, f), device_id_type=MESH,
        )

    def x_arrival(j, other):
        return pltpu.make_async_remote_copy(
            src_ref=x_send.at[j, other], dst_ref=x_recv.at[j, other],
            send_sem=x_out.at[j, other], recv_sem=x_in.at[j, other],
            device_id=(2 * block_row(OWNED[j]) + other, f), device_id_type=MESH,
        )

    quarter = part // 2

    def finish(j):
        chain(half - 1, j, *long_chain).wait_recv()
        chain(half - 2, j, *short_chain).wait_recv()
        tile = own(z(0), j)[...] + (recv_l[half - 1, j] + recv_s[half - 2, j])
        piece[block_row(OWNED[j])] = tile
        if j < SENT:
            stacked = jnp.concatenate([tile, pltpu.roll(tile, block - quarter, 1)], axis=0)
            turned = stacked.T
            for other in (0, 1):
                x_send[j, other] = turned[other * part : other * part + quarter, :]
                x_copy(j, other).start()

    def send_weights():
        w_send[f] = weights(f)
        w_recv[f] = weights(f)

        @pl.loop(1, trees)
        def _(r):
            owner = (f + r) % trees
            w_send[owner] = weights(owner)
            w_copy(r, owner, f).start()

    order = []
    for j in range(len(OWNED)):
        for k in range(half):
            order.append((k + LAG[j], k > 0, j, 0, k))
        for k in range(half - 1):
            order.append((k + LAG[j], True, j, 1, k))
        order.append((half + LAG[j], True, j, 2, half))
    order.sort()
    done = 1
    multiply(group_order[0])
    pl.semaphore_wait(barrier, trees + 1)
    for slot, _, j, kind, k in order:
        needed = 4 if k > 3 else 3 if k > 1 else 2 if (kind, k) != (0, 0) else 1
        while done < needed:
            multiply(group_order[done])
            done += 1
        if kind == 0:
            advance(k, j, *long_chain)
        elif kind == 1:
            advance(k, j, *short_chain)
        else:
            finish(j)
        if (j, kind, k) == (len(OWNED) - 1, 1, 3):
            send_weights()

    lane = lax.broadcasted_iota(jnp.int32, (quarter, block), 1)
    for j in range(SENT):
        for other in (0, 1):
            x_arrival(j, other).wait_recv()
        low = x_recv[j, 0]
        high = x_recv[j, 1]
        n = block_row(-OWNED[j])
        piece[n, :quarter, :] = jnp.where(lane < part, low, pltpu.roll(high, part, 1))
        piece[n, quarter:, :] = jnp.where(lane < part, pltpu.roll(low, part, 1), high)
    piece[nb] = jnp.zeros(piece.shape[1:], jnp.float32)

    def chosen(owner):
        index = jnp.int32(nb)
        for c in range(nb):
            first = anc_ref[c] - ANC_DEV * owner
            index = jnp.where((first >= 0) & (first < ANC_DEV), c, index)
        return piece[index]

    @pl.loop(1, trees)
    def _(r):
        owner = (f + r) % trees
        t_send[owner] = chosen(owner)
        t_copy(r, owner, f).start()

    def added(source, tile, totals):
        weight = w_recv[source]
        return tuple(totals[a] + weight[a : a + 1, :] * tile for a in range(ANC_DEV))

    zero = jnp.zeros(piece.shape[1:], jnp.float32)
    totals = added(f, chosen(f), (zero,) * ANC_DEV)

    def gather(r, totals):
        source = (f + trees - r) % trees
        w_copy(r, source, source).wait_recv()
        t_copy(r, source, source).wait_recv()
        return added(source, t_recv[source], totals)

    totals = lax.fori_loop(1, trees, gather, totals)
    for a in range(ANC_DEV):
        out_ref[a] = totals[a]

    for j in range(len(OWNED)):
        for k in range(half):
            chain(k, j, *long_chain).wait_send()
        for k in range(half - 1):
            chain(k, j, *short_chain).wait_send()
    for j in range(SENT):
        for other in (0, 1):
            x_copy(j, other).wait_send()

    @pl.loop(1, trees)
    def _(r):
        owner = (f + r) % trees
        w_copy(r, owner, f).wait_send()
        t_copy(r, owner, f).wait_send()


def solution(mesh):
    subs, trees = mesh.shape["subtree"], mesh.shape["forest"]

    def per_device(panels, pattern, child_map, ancestor_map):
        rows, depth = panels.shape[2:]
        nb = child_map.shape[2]
        block = rows // nb
        part = block // 2
        half = subs // 2
        owned = len(OWNED)
        dma = pltpu.SemaphoreType.DMA
        smem = pl.BlockSpec(memory_space=pltpu.SMEM)
        vmem = pl.BlockSpec(memory_space=pltpu.VMEM)
        f32 = jnp.float32
        out = pl.pallas_call(
            lambda *refs: kernel(subs, trees, *refs),
            name="assemble",
            out_shape=jax.ShapeDtypeStruct((ANC_DEV, part, block), f32),
            in_specs=[smem, smem, smem, pl.BlockSpec(memory_space=pl.ANY)],
            out_specs=vmem,
            scratch_shapes=[
                pltpu.VMEM((nb, block, depth), jnp.bfloat16),
                pltpu.VMEM((rows, depth), jnp.bfloat16),
                pltpu.VMEM((nb, rows, block), f32),
                pltpu.VMEM((half, owned, part, block), f32),
                pltpu.VMEM((half - 1, owned, part, block), f32),
                pltpu.VMEM((nb + 1, part, block), f32),
                pltpu.VMEM((SENT, 2, part // 2, block), f32),
                pltpu.VMEM((SENT, 2, part // 2, block), f32),
                pltpu.VMEM((trees, 8, block), f32),
                pltpu.VMEM((trees, 8, block), f32),
                pltpu.VMEM((trees, part, block), f32),
                pltpu.VMEM((trees, part, block), f32),
                dma((half, owned)), dma((half, owned)),
                dma((half - 1, owned)), dma((half - 1, owned)),
                dma((SENT, 2)), dma((SENT, 2)),
                dma((trees,)), dma((trees,)),
                dma((trees,)), dma((trees,)),
                dma(()),
            ],
            compiler_params=pltpu.CompilerParams(
                collective_id=0, has_side_effects=True, vmem_limit_bytes=60 * 2**20
            ),
        )(child_map[0, 0], pattern[0, 0], ancestor_map[0, 0], panels.reshape(nb, block, depth))
        return out[None]

    return jax.shard_map(
        per_device,
        mesh=mesh,
        in_specs=(
            P("subtree", "forest", None, None),
            P("subtree", "forest", None, None),
            P("subtree", "forest", None),
            P("subtree", "forest", None),
        ),
        out_specs=P("subtree", "forest", None, None),
        check_vma=False,
    )
```

```python
import jax
import jax.numpy as jnp
from jax import lax
from jax.experimental import pallas as pl
from jax.experimental.pallas import tpu as pltpu
from jax.sharding import PartitionSpec as P

MESH = pl.DeviceIdType.MESH
ANC_DEV = 3
OWNED = (5, 2, 1, 4, 0)
SENT = 3
LAG = (0, 0, 0, 1, 1)
STRIDE = 11


def kernel(
    subs, trees,
    child_ref, pattern_ref, anc_ref, panel_hbm, out_ref,
    panel_ref, rows, gram, recv_l, recv_s, piece, x_send, x_recv, w_send, w_recv, t_send, t_recv,
    l_out, l_in, s_out, s_in, x_out, x_in, w_out, w_in, t_out, t_in, panel_in, choice,
):
    nb = child_ref.shape[0]
    block = panel_hbm.shape[1]
    part = block // 2
    half = subs // 2
    s = lax.axis_index("subtree")
    f = lax.axis_index("forest")
    m = s // 2
    side = s % 2
    sigma = 1 - 2 * (f % 2)

    def z(offset):
        return (s + offset + 4 * subs) % subs

    def block_row(offset):
        return (m + offset + 4 * nb) % nb

    load = pltpu.make_async_copy(panel_hbm, panel_ref, panel_in)
    load.start()

    barrier = pltpu.get_barrier_semaphore()
    for step in (1, -1):
        pl.semaphore_signal(barrier, inc=1, device_id=(z(step), f), device_id_type=MESH)

    @pl.loop(1, trees)
    def _(r):
        pl.semaphore_signal(
            barrier, inc=1, device_id=(s, (f + r) % trees), device_id_type=MESH
        )

    slots = w_send.shape
    number = ANC_DEV * lax.broadcasted_iota(jnp.int32, slots, 0)
    number += lax.broadcasted_iota(jnp.int32, slots, 1)
    total = jnp.zeros(slots, jnp.float32)
    for c in range(nb):
        total += jnp.where(number == anc_ref[c], 1.0, 0.0)
    w_send[...] = total
    w_recv[f] = w_send[f]

    @pl.loop(0, trees)
    def _(owner):
        index = jnp.int32(nb)
        for c in range(nb):
            first = anc_ref[c] - ANC_DEV * owner
            index = jnp.where((first >= 0) & (first < ANC_DEV), c, index)
        choice[owner] = index

    piece[nb] = jnp.zeros(piece.shape[1:], jnp.float32)

    load.wait()

    @pl.loop(0, nb + 2)
    def _(place):
        to = place % nb
        source = jnp.int32(0)
        for i in range(nb):
            source = jnp.where(child_ref[i] == to, i, source)
        keep = jnp.int32(0)
        for i in range(nb):
            keep = jnp.where(child_ref[i] == to, pattern_ref[i, i], keep)
        chunk = panel_ref[source]
        rows[pl.ds(pl.multiple_of(place * block, block), block), :] = chunk * keep.astype(
            jnp.float32
        ).astype(jnp.bfloat16)

    def multiply(w, q):
        first = (s + half - 1 + 4 * w) % subs
        product = lax.dot_general(
            rows[pl.ds(pl.multiple_of(first * part, part), 4 * part), :],
            rows[q * 2 * block : (q + 1) * 2 * block, :],
            (((1,), (1,)), ((), ())),
            preferred_element_type=jnp.float32,
        )
        for h in (0, 1):
            gram[2 * q + h, 4 * w * part : 4 * (w + 1) * part, :] = product[
                :, h * block : (h + 1) * block
            ]

    def w_copy(r, owner, source):
        return pltpu.make_async_remote_copy(
            src_ref=w_send.at[owner], dst_ref=w_recv.at[source],
            send_sem=w_out.at[r], recv_sem=w_in.at[r],
            device_id=(s, owner), device_id_type=MESH,
        )

    def t_copy(r, owner, source):
        return pltpu.make_async_remote_copy(
            src_ref=t_send.at[owner], dst_ref=t_recv.at[source],
            send_sem=t_out.at[r], recv_sem=t_in.at[r],
            device_id=(s, owner), device_id_type=MESH,
        )

    def own(offset, j):
        at = (offset + 2 * subs - half + 1) % subs
        return gram.at[
            (z(offset) // 2 + OWNED[j]) % nb, pl.ds(pl.multiple_of(at * part, part), part), :
        ]

    def chain(k, j, buffers, outs, ins, direction, steps):
        if k == 0:
            source = own(direction * steps, j)
        else:
            source = buffers.at[k - 1, j]
        return pltpu.make_async_remote_copy(
            src_ref=source, dst_ref=buffers.at[k, j],
            send_sem=outs.at[k, j], recv_sem=ins.at[k, j],
            device_id=(z(direction), f), device_id_type=MESH,
        )

    def advance(k, j, buffers, outs, ins, direction, steps):
        if k > 0:
            chain(k - 1, j, buffers, outs, ins, direction, steps).wait_recv()
            buffers[k - 1, j] = buffers[k - 1, j] + own(direction * (steps - k), j)[...]
        chain(k, j, buffers, outs, ins, direction, steps).start()

    long_chain = (recv_l, l_out, l_in, sigma, half)
    short_chain = (recv_s, s_out, s_in, -sigma, half - 1)

    def x_copy(j, other):
        n = block_row(OWNED[j])
        return pltpu.make_async_remote_copy(
            src_ref=x_send.at[j, other], dst_ref=x_recv.at[j, side],
            send_sem=x_out.at[j, other], recv_sem=x_in.at[j, side],
            device_id=(2 * n + other, f), device_id_type=MESH,
        )

    def x_arrival(j, other):
        return pltpu.make_async_remote_copy(
            src_ref=x_send.at[j, other], dst_ref=x_recv.at[j, other],
            send_sem=x_out.at[j, other], recv_sem=x_in.at[j, other],
            device_id=(2 * block_row(OWNED[j]) + other, f), device_id_type=MESH,
        )

    quarter = part // 2

    def finish(j):
        chain(half - 1, j, *long_chain).wait_recv()
        chain(half - 2, j, *short_chain).wait_recv()
        tile = own(0, j)[...] + (recv_l[half - 1, j] + recv_s[half - 2, j])
        piece[block_row(OWNED[j])] = tile
        if j < SENT:
            stacked = jnp.concatenate([tile, pltpu.roll(tile, block - quarter, 1)], axis=0)
            turned = stacked.T
            for other in (0, 1):
                x_send[j, other] = turned[other * part : other * part + quarter, :]
                x_copy(j, other).start()

    def send_weights(low, high):
        @pl.loop(low, high)
        def _(r):
            owner = (f + r) % trees
            w_copy(r, owner, f).start()

    beside = {}
    for q in range(nb // 2):
        beside[1, q] = [(multiply, 1, q)]
        beside[2 + q // 2, 1 + 2 * (q % 2)] = [(multiply, 2, q)]
        beside[4 + q // 2, 1 + 2 * (q % 2)] = [
            (send_weights, max(1, trees * q // 4), trees * (q + 1) // 4)
        ]

    order = []
    for j in range(len(OWNED)):
        for k in range(half):
            order.append((k + LAG[j], j, 0, k))
        for k in range(half - 1):
            order.append((k + LAG[j], j, 1, k))
        order.append((half + LAG[j], j, 2, half))
    order.sort()
    for q in range(nb // 2):
        multiply(0, q)
    pl.semaphore_wait(barrier, trees + 1)
    for at, (slot, j, kind, k) in enumerate(order):
        if slot == 1 and order[at - 1][0] == 0:
            for q in range(nb // 2):
                multiply(3, q)
        if kind == 0:
            advance(k, j, *long_chain)
        elif kind == 1:
            advance(k, j, *short_chain)
        else:
            finish(j)
        if at + 1 == len(order) or order[at + 1][:2] != (slot, j):
            for work, *given in beside.pop((slot, j), []):
                work(*given)

    lane = lax.broadcasted_iota(jnp.int32, (quarter, block), 1)
    for j in range(SENT):
        for other in (0, 1):
            x_arrival(j, other).wait_recv()
        low = x_recv[j, 0]
        high = x_recv[j, 1]
        n = block_row(-OWNED[j])
        piece[n, :quarter, :] = jnp.where(lane < part, low, pltpu.roll(high, part, 1))
        piece[n, quarter:, :] = jnp.where(lane < part, pltpu.roll(low, part, 1), high)
    @pl.loop(1, trees)
    def _(r):
        owner = (f + STRIDE * r) % trees
        t_send[owner] = piece[choice[owner]]
        t_copy(r, owner, f).start()

    def added(source, tile, totals):
        weight = w_recv[source]
        return tuple(totals[a] + weight[a : a + 1, :] * tile for a in range(ANC_DEV))

    zero = jnp.zeros(piece.shape[1:], jnp.float32)
    totals = added(f, piece[choice[f]], (zero,) * ANC_DEV)

    def gather(r, totals):
        source = (f + STRIDE * (trees - r)) % trees
        t_copy(r, source, source).wait_recv()
        return added(source, t_recv[source], totals)

    @pl.loop(1, trees)
    def _(r):
        source = (f + trees - r) % trees
        w_copy(r, source, source).wait_recv()

    totals = lax.fori_loop(1, trees, gather, totals)
    for a in range(ANC_DEV):
        out_ref[a] = totals[a]

    for j in range(len(OWNED)):
        for k in range(half):
            chain(k, j, *long_chain).wait_send()
        for k in range(half - 1):
            chain(k, j, *short_chain).wait_send()
    for j in range(SENT):
        for other in (0, 1):
            x_copy(j, other).wait_send()

    @pl.loop(1, trees)
    def _(r):
        w_copy(r, (f + r) % trees, f).wait_send()
        t_copy(r, (f + STRIDE * r) % trees, f).wait_send()


def solution(mesh):
    subs, trees = mesh.shape["subtree"], mesh.shape["forest"]

    def per_device(panels, pattern, child_map, ancestor_map):
        rows, depth = panels.shape[2:]
        nb = child_map.shape[2]
        block = rows // nb
        part = block // 2
        half = subs // 2
        owned = len(OWNED)
        dma = pltpu.SemaphoreType.DMA
        smem = pl.BlockSpec(memory_space=pltpu.SMEM)
        vmem = pl.BlockSpec(memory_space=pltpu.VMEM)
        f32 = jnp.float32
        out = pl.pallas_call(
            lambda *refs: kernel(subs, trees, *refs),
            name="assemble",
            out_shape=jax.ShapeDtypeStruct((ANC_DEV, part, block), f32),
            in_specs=[smem, smem, smem, pl.BlockSpec(memory_space=pl.ANY)],
            out_specs=vmem,
            scratch_shapes=[
                pltpu.VMEM((nb, block, depth), jnp.bfloat16),
                pltpu.VMEM((rows + 2 * block, depth), jnp.bfloat16),
                pltpu.VMEM((nb, rows, block), f32),
                pltpu.VMEM((half, owned, part, block), f32),
                pltpu.VMEM((half - 1, owned, part, block), f32),
                pltpu.VMEM((nb + 1, part, block), f32),
                pltpu.VMEM((SENT, 2, part // 2, block), f32),
                pltpu.VMEM((SENT, 2, part // 2, block), f32),
                pltpu.VMEM((trees, 8, block), f32),
                pltpu.VMEM((trees, 8, block), f32),
                pltpu.VMEM((trees, part, block), f32),
                pltpu.VMEM((trees, part, block), f32),
                dma((half, owned)), dma((half, owned)),
                dma((half - 1, owned)), dma((half - 1, owned)),
                dma((SENT, 2)), dma((SENT, 2)),
                dma((trees,)), dma((trees,)),
                dma((trees,)), dma((trees,)),
                dma(()),
                pltpu.SMEM((trees,), jnp.int32),
            ],
            compiler_params=pltpu.CompilerParams(
                collective_id=0, has_side_effects=True, vmem_limit_bytes=60 * 2**20
            ),
        )(child_map[0, 0], pattern[0, 0], ancestor_map[0, 0], panels.reshape(nb, block, depth))
        return out[None]

    return jax.shard_map(
        per_device,
        mesh=mesh,
        in_specs=(
            P("subtree", "forest", None, None),
            P("subtree", "forest", None, None),
            P("subtree", "forest", None),
            P("subtree", "forest", None),
        ),
        out_specs=P("subtree", "forest", None, None),
        check_vma=False,
    )
```

```python
import jax
import jax.numpy as jnp
from jax import lax
from jax.experimental import pallas as pl
from jax.experimental.pallas import tpu as pltpu
from jax.sharding import PartitionSpec as P

MESH = pl.DeviceIdType.MESH
ANC_DEV = 3
OWNED = (5, 2, 1, 4, 0)
SENT = 3
LAG = (0, 0, 0, 1, 1)
STRIDE = 11


def kernel(
    subs, trees,
    child_ref, pattern_ref, anc_ref, panel_hbm, out_ref,
    panel_ref, rows, gram, recv_l, recv_s, piece, x_send, x_recv, w_send, w_recv, t_send, t_recv,
    l_out, l_in, s_out, s_in, x_out, x_in, w_out, w_in, t_out, t_in, panel_in, choice,
):
    nb = child_ref.shape[0]
    block = panel_hbm.shape[1]
    part = block // 2
    half = subs // 2
    s = lax.axis_index("subtree")
    f = lax.axis_index("forest")
    m = s // 2
    side = s % 2
    sigma = 1 - 2 * (f % 2)

    def z(offset):
        return (s + offset + 4 * subs) % subs

    def block_row(offset):
        return (m + offset + 4 * nb) % nb

    load = pltpu.make_async_copy(panel_hbm, panel_ref, panel_in)
    load.start()

    barrier = pltpu.get_barrier_semaphore()
    for step in (1, -1):
        pl.semaphore_signal(barrier, inc=1, device_id=(z(step), f), device_id_type=MESH)

    @pl.loop(1, trees)
    def _(r):
        pl.semaphore_signal(
            barrier, inc=1, device_id=(s, (f + r) % trees), device_id_type=MESH
        )

    slots = w_send.shape
    number = ANC_DEV * lax.broadcasted_iota(jnp.int32, slots, 0)
    number += lax.broadcasted_iota(jnp.int32, slots, 1)
    total = jnp.zeros(slots, jnp.float32)
    for c in range(nb):
        total += jnp.where(number == anc_ref[c], 1.0, 0.0)
    w_send[...] = total
    w_recv[f] = w_send[f]

    @pl.loop(0, trees)
    def _(owner):
        index = jnp.int32(nb)
        for c in range(nb):
            first = anc_ref[c] - ANC_DEV * owner
            index = jnp.where((first >= 0) & (first < ANC_DEV), c, index)
        choice[owner] = index

    piece[nb] = jnp.zeros(piece.shape[1:], jnp.float32)

    load.wait()

    @pl.loop(0, nb + 2)
    def _(place):
        to = place % nb
        source = jnp.int32(0)
        for i in range(nb):
            source = jnp.where(child_ref[i] == to, i, source)
        keep = jnp.int32(0)
        for i in range(nb):
            keep = jnp.where(child_ref[i] == to, pattern_ref[i, i], keep)
        chunk = panel_ref[source]
        rows[pl.ds(pl.multiple_of(place * block, block), block), :] = chunk * keep.astype(
            jnp.float32
        ).astype(jnp.bfloat16)

    def multiply(w, q):
        first = (s + half - 1 + 4 * w) % subs
        product = lax.dot_general(
            rows[pl.ds(pl.multiple_of(first * part, part), 4 * part), :],
            rows[q * 2 * block : (q + 1) * 2 * block, :],
            (((1,), (1,)), ((), ())),
            preferred_element_type=jnp.float32,
        )
        for h in (0, 1):
            gram[2 * q + h, 4 * w * part : 4 * (w + 1) * part, :] = product[
                :, h * block : (h + 1) * block
            ]

    def w_copy(r, owner, source):
        return pltpu.make_async_remote_copy(
            src_ref=w_send.at[owner], dst_ref=w_recv.at[source],
            send_sem=w_out.at[r], recv_sem=w_in.at[r],
            device_id=(s, owner), device_id_type=MESH,
        )

    def t_copy(r, owner, source):
        return pltpu.make_async_remote_copy(
            src_ref=t_send.at[owner], dst_ref=t_recv.at[source],
            send_sem=t_out.at[r], recv_sem=t_in.at[r],
            device_id=(s, owner), device_id_type=MESH,
        )

    def own(offset, j):
        at = (offset + 2 * subs - half + 1) % subs
        return gram.at[
            (z(offset) // 2 + OWNED[j]) % nb, pl.ds(pl.multiple_of(at * part, part), part), :
        ]

    def chain(k, j, buffers, outs, ins, direction, steps):
        if k == 0:
            source = own(direction * steps, j)
        else:
            source = buffers.at[k - 1, j]
        return pltpu.make_async_remote_copy(
            src_ref=source, dst_ref=buffers.at[k, j],
            send_sem=outs.at[k, j], recv_sem=ins.at[k, j],
            device_id=(z(direction), f), device_id_type=MESH,
        )

    def advance(k, j, buffers, outs, ins, direction, steps):
        if k > 0:
            chain(k - 1, j, buffers, outs, ins, direction, steps).wait_recv()
            buffers[k - 1, j] = buffers[k - 1, j] + own(direction * (steps - k), j)[...]
        chain(k, j, buffers, outs, ins, direction, steps).start()

    long_chain = (recv_l, l_out, l_in, sigma, half)
    short_chain = (recv_s, s_out, s_in, -sigma, half - 1)

    def x_copy(j, other):
        n = block_row(OWNED[j])
        return pltpu.make_async_remote_copy(
            src_ref=x_send.at[j, other], dst_ref=x_recv.at[j, side],
            send_sem=x_out.at[j, other], recv_sem=x_in.at[j, side],
            device_id=(2 * n + other, f), device_id_type=MESH,
        )

    def x_arrival(j, other):
        return pltpu.make_async_remote_copy(
            src_ref=x_send.at[j, other], dst_ref=x_recv.at[j, other],
            send_sem=x_out.at[j, other], recv_sem=x_in.at[j, other],
            device_id=(2 * block_row(OWNED[j]) + other, f), device_id_type=MESH,
        )

    quarter = part // 2

    def finish(j):
        chain(half - 1, j, *long_chain).wait_recv()
        chain(half - 2, j, *short_chain).wait_recv()
        tile = own(0, j)[...] + (recv_l[half - 1, j] + recv_s[half - 2, j])
        piece[block_row(OWNED[j])] = tile
        if j < SENT:
            stacked = jnp.concatenate([tile, pltpu.roll(tile, block - quarter, 1)], axis=0)
            turned = stacked.T
            for other in (0, 1):
                x_send[j, other] = turned[other * part : other * part + quarter, :]
                x_copy(j, other).start()

    def send_weights(low, high):
        @pl.loop(low, high)
        def _(r):
            owner = (f + r) % trees
            w_copy(r, owner, f).start()

    beside = {}
    for q in range(nb // 2):
        beside[1, q] = [(multiply, 1, q)]
        beside[2 + q // 2, 1 + 2 * (q % 2)] = [(multiply, 2, q)]
        beside[4 + q // 2, 1 + 2 * (q % 2)] = [
            (send_weights, max(1, trees * q // 4), trees * (q + 1) // 4)
        ]

    order = []
    for j in range(len(OWNED)):
        for k in range(half):
            order.append((k + LAG[j], j, 0, k))
        for k in range(half - 1):
            order.append((k + LAG[j], j, 1, k))
        order.append((half + LAG[j], j, 2, half))
    order.sort()
    for q in range(nb // 2):
        multiply(0, q)
    pl.semaphore_wait(barrier, trees + 1)
    for at, (slot, j, kind, k) in enumerate(order):
        if slot == 1 and order[at - 1][0] == 0:
            for q in range(nb // 2):
                multiply(3, q)
        if kind == 0:
            advance(k, j, *long_chain)
        elif kind == 1:
            advance(k, j, *short_chain)
        else:
            finish(j)
        if at + 1 == len(order) or order[at + 1][:2] != (slot, j):
            for work, *given in beside.pop((slot, j), []):
                work(*given)

    lane = lax.broadcasted_iota(jnp.int32, (quarter, block), 1)
    for j in range(SENT):
        for other in (0, 1):
            x_arrival(j, other).wait_recv()
        low = x_recv[j, 0]
        high = x_recv[j, 1]
        n = block_row(-OWNED[j])
        piece[n, :quarter, :] = jnp.where(lane < part, low, pltpu.roll(high, part, 1))
        piece[n, quarter:, :] = jnp.where(lane < part, pltpu.roll(low, part, 1), high)
    @pl.loop(1, trees)
    def _(r):
        owner = (f + STRIDE * r) % trees
        t_send[owner] = piece[choice[owner]]
        t_copy(r, owner, f).start()

    def added(source, tile, totals):
        weight = w_recv[source]
        return tuple(totals[a] + weight[a : a + 1, :] * tile for a in range(ANC_DEV))

    zero = jnp.zeros(piece.shape[1:], jnp.float32)
    totals = added(f, piece[choice[f]], (zero,) * ANC_DEV)

    def gather(r, totals):
        source = (f + STRIDE * (trees - r)) % trees
        t_copy(r, source, source).wait_recv()
        return added(source, t_recv[source], totals)

    @pl.loop(1, trees)
    def _(r):
        source = (f + trees - r) % trees
        w_copy(r, source, source).wait_recv()

    totals = lax.fori_loop(1, trees, gather, totals)
    for a in range(ANC_DEV):
        out_ref[a] = totals[a]

    for j in range(len(OWNED)):
        for k in range(half):
            chain(k, j, *long_chain).wait_send()
        for k in range(half - 1):
            chain(k, j, *short_chain).wait_send()
    for j in range(SENT):
        for other in (0, 1):
            x_copy(j, other).wait_send()

    @pl.loop(1, trees)
    def _(r):
        w_copy(r, (f + r) % trees, f).wait_send()
        t_copy(r, (f + STRIDE * r) % trees, f).wait_send()


def solution(mesh):
    subs, trees = mesh.shape["subtree"], mesh.shape["forest"]

    def per_device(panels, pattern, child_map, ancestor_map):
        rows, depth = panels.shape[2:]
        nb = child_map.shape[2]
        block = rows // nb
        part = block // 2
        half = subs // 2
        owned = len(OWNED)
        dma = pltpu.SemaphoreType.DMA
        smem = pl.BlockSpec(memory_space=pltpu.SMEM)
        vmem = pl.BlockSpec(memory_space=pltpu.VMEM)
        f32 = jnp.float32
        out = pl.pallas_call(
            lambda *refs: kernel(subs, trees, *refs),
            name="assemble",
            out_shape=pltpu.VMEM((ANC_DEV, part, block), f32),
            in_specs=[smem, smem, smem, pl.BlockSpec(memory_space=pl.ANY)],
            out_specs=vmem,
            scratch_shapes=[
                pltpu.VMEM((nb, block, depth), jnp.bfloat16),
                pltpu.VMEM((rows + 2 * block, depth), jnp.bfloat16),
                pltpu.VMEM((nb, rows, block), f32),
                pltpu.VMEM((half, owned, part, block), f32),
                pltpu.VMEM((half - 1, owned, part, block), f32),
                pltpu.VMEM((nb + 1, part, block), f32),
                pltpu.VMEM((SENT, 2, part // 2, block), f32),
                pltpu.VMEM((SENT, 2, part // 2, block), f32),
                pltpu.VMEM((trees, 8, block), f32),
                pltpu.VMEM((trees, 8, block), f32),
                pltpu.VMEM((trees, part, block), f32),
                pltpu.VMEM((trees, part, block), f32),
                dma((half, owned)), dma((half, owned)),
                dma((half - 1, owned)), dma((half - 1, owned)),
                dma((SENT, 2)), dma((SENT, 2)),
                dma((trees,)), dma((trees,)),
                dma((trees,)), dma((trees,)),
                dma(()),
                pltpu.SMEM((trees,), jnp.int32),
            ],
            compiler_params=pltpu.CompilerParams(
                collective_id=0, has_side_effects=True, vmem_limit_bytes=60 * 2**20
            ),
        )(child_map[0, 0], pattern[0, 0], ancestor_map[0, 0], panels.reshape(nb, block, depth))
        return out[None]

    return jax.shard_map(
        per_device,
        mesh=mesh,
        in_specs=(
            P("subtree", "forest", None, None),
            P("subtree", "forest", None, None),
            P("subtree", "forest", None),
            P("subtree", "forest", None),
        ),
        out_specs=P("subtree", "forest", None, None),
        check_vma=False,
    )
```

```python
import jax
import jax.numpy as jnp
from jax import lax
from jax.experimental import pallas as pl
from jax.experimental.pallas import tpu as pltpu
from jax.sharding import PartitionSpec as P

MESH = pl.DeviceIdType.MESH
ANC_DEV = 3
OWNED = (4, 5, 2, 1, 0)
SENT = (1, 2, 3)
LAG = (0, 0, 0, 0, 0)
STRIDE = 11


def kernel(
    subs, trees,
    child_ref, pattern_ref, anc_ref, panel_hbm, out_ref,
    panel_ref, rows, gram, recv_l, recv_s, piece, x_send, x_recv, w_send, w_recv, t_send, t_recv,
    l_out, l_in, s_out, s_in, x_out, x_in, w_out, w_in, t_out, t_in, panel_in, choice,
    first_l, first_s, y_own, y_send, y_recv, y_out, y_in,
):
    nb = child_ref.shape[0]
    block = panel_hbm.shape[1]
    part = block // 2
    half = subs // 2
    s = lax.axis_index("subtree")
    f = lax.axis_index("forest")
    m = s // 2
    side = s % 2
    sigma = 1 - 2 * (f % 2)

    def z(offset):
        return (s + offset + 4 * subs) % subs

    def block_row(offset):
        return (m + offset + 4 * nb) % nb

    load = pltpu.make_async_copy(panel_hbm, panel_ref, panel_in)
    load.start()

    barrier = pltpu.get_barrier_semaphore()
    for step in (1, -1):
        pl.semaphore_signal(barrier, inc=1, device_id=(z(step), f), device_id_type=MESH)

    @pl.loop(1, trees)
    def _(r):
        pl.semaphore_signal(
            barrier, inc=1, device_id=(s, (f + r) % trees), device_id_type=MESH
        )

    slots = w_send.shape
    number = ANC_DEV * lax.broadcasted_iota(jnp.int32, slots, 0)
    number += lax.broadcasted_iota(jnp.int32, slots, 1)
    total = jnp.zeros(slots, jnp.float32)
    for c in range(nb):
        total += jnp.where(number == anc_ref[c], 1.0, 0.0)
    w_send[...] = total
    w_recv[f] = w_send[f]

    @pl.loop(0, trees)
    def _(owner):
        index = jnp.int32(nb)
        for c in range(nb):
            first = anc_ref[c] - ANC_DEV * owner
            index = jnp.where((first >= 0) & (first < ANC_DEV), c, index)
        choice[owner] = index

    piece[nb] = jnp.zeros(piece.shape[1:], jnp.float32)

    load.wait()

    @pl.loop(0, nb + 2)
    def _(place):
        to = place % nb
        source = jnp.int32(0)
        for i in range(nb):
            source = jnp.where(child_ref[i] == to, i, source)
        keep = jnp.int32(0)
        for i in range(nb):
            keep = jnp.where(child_ref[i] == to, pattern_ref[i, i], keep)
        chunk = panel_ref[source]
        rows[pl.ds(pl.multiple_of(place * block, block), block), :] = chunk * keep.astype(
            jnp.float32
        ).astype(jnp.bfloat16)

    def multiply(w, q):
        first = (s + half - 1 + 4 * w) % subs
        product = lax.dot_general(
            rows[pl.ds(pl.multiple_of(first * part, part), 4 * part), :],
            rows[q * 2 * block : (q + 1) * 2 * block, :],
            (((1,), (1,)), ((), ())),
            preferred_element_type=jnp.float32,
        )
        for h in (0, 1):
            gram[2 * q + h, 4 * w * part : 4 * (w + 1) * part, :] = product[
                :, h * block : (h + 1) * block
            ]

    def w_copy(r, owner, source):
        return pltpu.make_async_remote_copy(
            src_ref=w_send.at[owner], dst_ref=w_recv.at[source],
            send_sem=w_out.at[r], recv_sem=w_in.at[r],
            device_id=(s, owner), device_id_type=MESH,
        )

    def t_copy(r, owner, source):
        return pltpu.make_async_remote_copy(
            src_ref=t_send.at[owner], dst_ref=t_recv.at[source],
            send_sem=t_out.at[r], recv_sem=t_in.at[r],
            device_id=(s, owner), device_id_type=MESH,
        )

    def own(offset, j):
        at = (offset + 2 * subs - half + 1) % subs
        return gram.at[
            (z(offset) // 2 + OWNED[j]) % nb, pl.ds(pl.multiple_of(at * part, part), part), :
        ]

    quarter = part // 2
    lane = lax.broadcasted_iota(jnp.int32, (quarter, block), 1)

    def half_of(offset):
        row, its_side = z(offset) // 2, z(offset) % 2
        upper = row // (nb // 2)
        return its_side * (1 - upper) + (1 - its_side) * upper

    def turn(value):
        return pltpu.roll(value, part, 1)

    def mine(offset, j):
        tile = own(offset, j)[...]
        if j > 0:
            return tile
        which = jnp.full(tile.shape, half_of(offset), jnp.int32)
        tile = jnp.where(which == 0, tile, turn(tile))
        return jnp.where(lane < part, tile[:quarter], turn(tile[quarter:]))

    def at_tile(j):
        return pl.ds(0, quarter) if j == 0 else pl.ds(quarter + part * (j - 1), part)

    def chain(k, j, first, buffers, outs, ins, direction, steps):
        if k > 0:
            source = buffers.at[k - 1, at_tile(j)]
        elif j > 0:
            source = own(direction * steps, j)
        else:
            source = first
        return pltpu.make_async_remote_copy(
            src_ref=source, dst_ref=buffers.at[k, at_tile(j)],
            send_sem=outs.at[k, j], recv_sem=ins.at[k, j],
            device_id=(z(direction), f), device_id_type=MESH,
        )

    def advance(k, j, first, buffers, outs, ins, direction, steps):
        if k > 0:
            term = mine(direction * (steps - k), j)
            chain(k - 1, j, first, buffers, outs, ins, direction, steps).wait_recv()
            buffers[k - 1, at_tile(j)] = buffers[k - 1, at_tile(j)] + term
        elif j == 0:
            first[...] = mine(direction * steps, j)
        chain(k, j, first, buffers, outs, ins, direction, steps).start()

    long_chain = (first_l, recv_l, l_out, l_in, sigma, half)
    short_chain = (first_s, recv_s, s_out, s_in, -sigma, half - 1)
    my_half = half_of(0)
    y_copy = pltpu.make_async_remote_copy(
        src_ref=y_send, dst_ref=y_recv, send_sem=y_out, recv_sem=y_in,
        device_id=(2 * block_row(nb // 2) + my_half, f), device_id_type=MESH,
    )

    def x_copy(j, other):
        n = block_row(OWNED[j])
        return pltpu.make_async_remote_copy(
            src_ref=x_send.at[j - 1, other], dst_ref=x_recv.at[j - 1, side],
            send_sem=x_out.at[j - 1, other], recv_sem=x_in.at[j - 1, side],
            device_id=(2 * n + other, f), device_id_type=MESH,
        )

    def x_arrival(j, other):
        return pltpu.make_async_remote_copy(
            src_ref=x_send.at[j - 1, other], dst_ref=x_recv.at[j - 1, other],
            send_sem=x_out.at[j - 1, other], recv_sem=x_in.at[j - 1, other],
            device_id=(2 * block_row(OWNED[j]) + other, f), device_id_type=MESH,
        )

    def finish(j):
        term = mine(0, j)
        chain(half - 1, j, *long_chain).wait_recv()
        chain(half - 2, j, *short_chain).wait_recv()
        tile = term + (recv_l[half - 1, at_tile(j)] + recv_s[half - 2, at_tile(j)])
        if j == 0:
            y_own[...] = tile
            tile = jnp.concatenate([tile, turn(tile)], axis=0)
        else:
            piece[block_row(OWNED[j])] = tile
        if j == 0 or j in SENT:
            stacked = jnp.concatenate([tile, pltpu.roll(tile, block - quarter, 1)], axis=0)
            turned = stacked.T
        if j == 0:
            y_send[...] = turned[:quarter, :]
            y_copy.start()
        elif j in SENT:
            for other in (0, 1):
                x_send[j - 1, other] = turned[other * part : other * part + quarter, :]
                x_copy(j, other).start()

    def send_weights(low, high):
        @pl.loop(low, high)
        def _(r):
            owner = (f + r) % trees
            w_copy(r, owner, f).start()

    beside = {}
    for q in range(nb // 2):
        beside[1, q] = [(multiply, 1, q)]
        beside[2 + q // 2, 1 + 2 * (q % 2)] = [(multiply, 2, q)]
        beside[4 + q // 2, 1 + 2 * (q % 2)] = [
            (send_weights, max(1, trees * q // 4), trees * (q + 1) // 4)
        ]

    order = []
    for j in range(len(OWNED)):
        for k in range(half):
            order.append((k + LAG[j], j, 0, k))
        for k in range(half - 1):
            order.append((k + LAG[j], j, 1, k))
        order.append((half + LAG[j], j, 2, half))
    order.sort()
    for q in range(nb // 2):
        multiply(0, q)
    pl.semaphore_wait(barrier, trees + 1)
    for at, (slot, j, kind, k) in enumerate(order):
        if slot == 1 and order[at - 1][0] == 0:
            for q in range(nb // 2):
                multiply(3, q)
        if kind == 0:
            advance(k, j, *long_chain)
        elif kind == 1:
            advance(k, j, *short_chain)
        else:
            finish(j)
        if at + 1 == len(order) or order[at + 1][:2] != (slot, j):
            for work, *given in beside.pop((slot, j), []):
                work(*given)

    def put(n, low, high):
        piece[n, :quarter, :] = jnp.where(lane < part, low, turn(high))
        piece[n, quarter:, :] = jnp.where(lane < part, turn(low), high)

    for j in reversed(SENT):
        for other in (0, 1):
            x_arrival(j, other).wait_recv()
        put(block_row(-OWNED[j]), x_recv[j - 1, 0], x_recv[j - 1, 1])
    y_copy.wait_recv()
    which = jnp.full(lane.shape, my_half, jnp.int32)
    put(
        block_row(nb // 2),
        jnp.where(which == 0, y_own[...], y_recv[...]),
        jnp.where(which == 0, y_recv[...], y_own[...]),
    )

    @pl.loop(1, trees)
    def _(r):
        owner = (f + STRIDE * r) % trees
        t_send[owner] = piece[choice[owner]]
        t_copy(r, owner, f).start()

    def added(source, tile, totals):
        weight = w_recv[source]
        return tuple(totals[a] + weight[a : a + 1, :] * tile for a in range(ANC_DEV))

    zero = jnp.zeros(piece.shape[1:], jnp.float32)
    totals = added(f, piece[choice[f]], (zero,) * ANC_DEV)

    def gather(r, totals):
        source = (f + STRIDE * (trees - r)) % trees
        t_copy(r, source, source).wait_recv()
        return added(source, t_recv[source], totals)

    @pl.loop(1, trees)
    def _(r):
        source = (f + trees - r) % trees
        w_copy(r, source, source).wait_recv()

    totals = lax.fori_loop(1, trees, gather, totals)
    for a in range(ANC_DEV):
        out_ref[a] = totals[a]

    for j in range(len(OWNED)):
        for k in range(half):
            chain(k, j, *long_chain).wait_send()
        for k in range(half - 1):
            chain(k, j, *short_chain).wait_send()
    y_copy.wait_send()
    for j in SENT:
        for other in (0, 1):
            x_copy(j, other).wait_send()

    @pl.loop(1, trees)
    def _(r):
        w_copy(r, (f + r) % trees, f).wait_send()
        t_copy(r, (f + STRIDE * r) % trees, f).wait_send()


def solution(mesh):
    subs, trees = mesh.shape["subtree"], mesh.shape["forest"]

    def per_device(panels, pattern, child_map, ancestor_map):
        rows, depth = panels.shape[2:]
        nb = child_map.shape[2]
        block = rows // nb
        part = block // 2
        half = subs // 2
        owned = len(OWNED)
        dma = pltpu.SemaphoreType.DMA
        smem = pl.BlockSpec(memory_space=pltpu.SMEM)
        vmem = pl.BlockSpec(memory_space=pltpu.VMEM)
        f32 = jnp.float32
        out = pl.pallas_call(
            lambda *refs: kernel(subs, trees, *refs),
            name="assemble",
            out_shape=pltpu.VMEM((ANC_DEV, part, block), f32),
            in_specs=[smem, smem, smem, pl.BlockSpec(memory_space=pl.ANY)],
            out_specs=vmem,
            scratch_shapes=[
                pltpu.VMEM((nb, block, depth), jnp.bfloat16),
                pltpu.VMEM((rows + 2 * block, depth), jnp.bfloat16),
                pltpu.VMEM((nb, rows, block), f32),
                pltpu.VMEM((half, part * owned - part // 2, block), f32),
                pltpu.VMEM((half - 1, part * owned - part // 2, block), f32),
                pltpu.VMEM((nb + 1, part, block), f32),
                pltpu.VMEM((len(SENT), 2, part // 2, block), f32),
                pltpu.VMEM((len(SENT), 2, part // 2, block), f32),
                pltpu.VMEM((trees, 8, block), f32),
                pltpu.VMEM((trees, 8, block), f32),
                pltpu.VMEM((trees, part, block), f32),
                pltpu.VMEM((trees, part, block), f32),
                dma((half, owned)), dma((half, owned)),
                dma((half - 1, owned)), dma((half - 1, owned)),
                dma((len(SENT), 2)), dma((len(SENT), 2)),
                dma((trees,)), dma((trees,)),
                dma((trees,)), dma((trees,)),
                dma(()),
                pltpu.SMEM((trees,), jnp.int32),
                pltpu.VMEM((part // 2, block), f32),
                pltpu.VMEM((part // 2, block), f32),
                pltpu.VMEM((part // 2, block), f32),
                pltpu.VMEM((part // 2, block), f32),
                pltpu.VMEM((part // 2, block), f32),
                dma(()), dma(()),
            ],
            compiler_params=pltpu.CompilerParams(
                collective_id=0, has_side_effects=True, vmem_limit_bytes=60 * 2**20
            ),
        )(child_map[0, 0], pattern[0, 0], ancestor_map[0, 0], panels.reshape(nb, block, depth))
        return out[None]

    return jax.shard_map(
        per_device,
        mesh=mesh,
        in_specs=(
            P("subtree", "forest", None, None),
            P("subtree", "forest", None, None),
            P("subtree", "forest", None),
            P("subtree", "forest", None),
        ),
        out_specs=P("subtree", "forest", None, None),
        check_vma=False,
    )
```

```python
import jax
import jax.numpy as jnp
from jax import lax
from jax.experimental import pallas as pl
from jax.experimental.pallas import tpu as pltpu
from jax.sharding import PartitionSpec as P

MESH = pl.DeviceIdType.MESH
ANC_DEV = 3
OWNED = (4, 5, 2, 1, 0)
SENT = (1, 2, 3)
LAG = (0, 0, 0, 0, 0)


def kernel(
    subs, trees,
    child_ref, pattern_ref, anc_ref, panel_hbm, out_ref,
    panel_ref, rows, gram, recv_l, recv_s, piece, x_send, x_recv, w_send, w_recv, t_send, t_recv,
    l_out, l_in, s_out, s_in, x_out, x_in, w_out, w_in, t_out, t_in, panel_in, choice,
    first_l, first_s, y_own, y_send, y_recv, y_out, y_in,
):
    nb = child_ref.shape[0]
    block = panel_hbm.shape[1]
    part = block // 2
    half = subs // 2
    s = lax.axis_index("subtree")
    f = lax.axis_index("forest")
    m = s // 2
    side = s % 2
    sigma = 1 - 2 * (f % 2)

    def z(offset):
        return (s + offset + 4 * subs) % subs

    def block_row(offset):
        return (m + offset + 4 * nb) % nb

    load = pltpu.make_async_copy(panel_hbm, panel_ref, panel_in)
    load.start()

    barrier = pltpu.get_barrier_semaphore()
    for step in (1, -1):
        pl.semaphore_signal(barrier, inc=1, device_id=(z(step), f), device_id_type=MESH)

    @pl.loop(1, trees)
    def _(r):
        pl.semaphore_signal(
            barrier, inc=1, device_id=(s, (f + r) % trees), device_id_type=MESH
        )

    slots = w_send.shape
    number = ANC_DEV * lax.broadcasted_iota(jnp.int32, slots, 0)
    number += lax.broadcasted_iota(jnp.int32, slots, 1)
    total = jnp.zeros(slots, jnp.float32)
    for c in range(nb):
        total += jnp.where(number == anc_ref[c], 1.0, 0.0)
    w_send[...] = total
    w_recv[f] = w_send[f]

    @pl.loop(0, trees)
    def _(owner):
        index = jnp.int32(nb)
        for c in range(nb):
            first = anc_ref[c] - ANC_DEV * owner
            index = jnp.where((first >= 0) & (first < ANC_DEV), c, index)
        choice[owner] = index

    piece[nb] = jnp.zeros(piece.shape[1:], jnp.float32)

    load.wait()

    @pl.loop(0, nb + 2)
    def _(place):
        to = place % nb
        source = jnp.int32(0)
        for i in range(nb):
            source = jnp.where(child_ref[i] == to, i, source)
        keep = jnp.int32(0)
        for i in range(nb):
            keep = jnp.where(child_ref[i] == to, pattern_ref[i, i], keep)
        chunk = panel_ref[source]
        rows[pl.ds(pl.multiple_of(place * block, block), block), :] = chunk * keep.astype(
            jnp.float32
        ).astype(jnp.bfloat16)

    def multiply(w, q):
        first = (s + half - 1 + 4 * w) % subs
        product = lax.dot_general(
            rows[pl.ds(pl.multiple_of(first * part, part), 4 * part), :],
            rows[q * 2 * block : (q + 1) * 2 * block, :],
            (((1,), (1,)), ((), ())),
            preferred_element_type=jnp.float32,
        )
        for h in (0, 1):
            gram[2 * q + h, 4 * w * part : 4 * (w + 1) * part, :] = product[
                :, h * block : (h + 1) * block
            ]

    def w_copy(r, owner, source):
        return pltpu.make_async_remote_copy(
            src_ref=w_send.at[owner], dst_ref=w_recv.at[source],
            send_sem=w_out.at[r], recv_sem=w_in.at[r],
            device_id=(s, owner), device_id_type=MESH,
        )

    def t_copy(r, owner, source):
        return pltpu.make_async_remote_copy(
            src_ref=t_send.at[owner], dst_ref=t_recv.at[source],
            send_sem=t_out.at[r], recv_sem=t_in.at[r],
            device_id=(s, owner), device_id_type=MESH,
        )

    def own(offset, j):
        at = (offset + 2 * subs - half + 1) % subs
        return gram.at[
            (z(offset) // 2 + OWNED[j]) % nb, pl.ds(pl.multiple_of(at * part, part), part), :
        ]

    quarter = part // 2
    lane = lax.broadcasted_iota(jnp.int32, (quarter, block), 1)

    def half_of(offset):
        row, its_side = z(offset) // 2, z(offset) % 2
        upper = row // (nb // 2)
        return its_side * (1 - upper) + (1 - its_side) * upper

    def turn(value):
        return pltpu.roll(value, part, 1)

    def mine(offset, j):
        tile = own(offset, j)[...]
        if j > 0:
            return tile
        which = jnp.full(tile.shape, half_of(offset), jnp.int32)
        tile = jnp.where(which == 0, tile, turn(tile))
        return jnp.where(lane < part, tile[:quarter], turn(tile[quarter:]))

    def at_tile(j):
        return pl.ds(0, quarter) if j == 0 else pl.ds(quarter + part * (j - 1), part)

    def chain(k, j, first, buffers, outs, ins, direction, steps):
        if k > 0:
            source = buffers.at[k - 1, at_tile(j)]
        elif j > 0:
            source = own(direction * steps, j)
        else:
            source = first
        return pltpu.make_async_remote_copy(
            src_ref=source, dst_ref=buffers.at[k, at_tile(j)],
            send_sem=outs.at[k, j], recv_sem=ins.at[k, j],
            device_id=(z(direction), f), device_id_type=MESH,
        )

    def advance(k, j, first, buffers, outs, ins, direction, steps):
        if k > 0:
            term = mine(direction * (steps - k), j)
            chain(k - 1, j, first, buffers, outs, ins, direction, steps).wait_recv()
            buffers[k - 1, at_tile(j)] = buffers[k - 1, at_tile(j)] + term
        elif j == 0:
            first[...] = mine(direction * steps, j)
        chain(k, j, first, buffers, outs, ins, direction, steps).start()

    long_chain = (first_l, recv_l, l_out, l_in, sigma, half)
    short_chain = (first_s, recv_s, s_out, s_in, -sigma, half - 1)
    my_half = half_of(0)
    y_copy = pltpu.make_async_remote_copy(
        src_ref=y_send, dst_ref=y_recv, send_sem=y_out, recv_sem=y_in,
        device_id=(2 * block_row(nb // 2) + my_half, f), device_id_type=MESH,
    )

    def x_copy(j, other):
        n = block_row(OWNED[j])
        return pltpu.make_async_remote_copy(
            src_ref=x_send.at[j - 1, other], dst_ref=x_recv.at[j - 1, side],
            send_sem=x_out.at[j - 1, other], recv_sem=x_in.at[j - 1, side],
            device_id=(2 * n + other, f), device_id_type=MESH,
        )

    def x_arrival(j, other):
        return pltpu.make_async_remote_copy(
            src_ref=x_send.at[j - 1, other], dst_ref=x_recv.at[j - 1, other],
            send_sem=x_out.at[j - 1, other], recv_sem=x_in.at[j - 1, other],
            device_id=(2 * block_row(OWNED[j]) + other, f), device_id_type=MESH,
        )

    def finish(j):
        term = mine(0, j)
        chain(half - 1, j, *long_chain).wait_recv()
        chain(half - 2, j, *short_chain).wait_recv()
        tile = term + (recv_l[half - 1, at_tile(j)] + recv_s[half - 2, at_tile(j)])
        if j == 0:
            y_own[...] = tile
            tile = jnp.concatenate([tile, turn(tile)], axis=0)
        else:
            piece[block_row(OWNED[j])] = tile
        if j == 0 or j in SENT:
            stacked = jnp.concatenate([tile, pltpu.roll(tile, block - quarter, 1)], axis=0)
            turned = stacked.T
        if j == 0:
            y_send[...] = turned[:quarter, :]
            y_copy.start()
        elif j in SENT:
            for other in (0, 1):
                x_send[j - 1, other] = turned[other * part : other * part + quarter, :]
                x_copy(j, other).start()

    def send_weights(low, high):
        @pl.loop(low, high)
        def _(r):
            owner = (f + r) % trees
            w_copy(r, owner, f).start()

    beside = {}
    for q in range(nb // 2):
        beside[1, q] = [(multiply, 1, q)]
        beside[2 + q // 2, 1 + 2 * (q % 2)] = [(multiply, 2, q)]
        beside[4 + q // 2, 1 + 2 * (q % 2)] = [
            (send_weights, max(1, trees * q // 4), trees * (q + 1) // 4)
        ]

    order = []
    for j in range(len(OWNED)):
        for k in range(half):
            order.append((k + LAG[j], j, 0, k))
        for k in range(half - 1):
            order.append((k + LAG[j], j, 1, k))
        order.append((half + LAG[j], j, 2, half))
    order.sort()
    for q in range(nb // 2):
        multiply(0, q)
    pl.semaphore_wait(barrier, trees + 1)
    for at, (slot, j, kind, k) in enumerate(order):
        if slot == 1 and order[at - 1][0] == 0:
            for q in range(nb // 2):
                multiply(3, q)
        if kind == 0:
            advance(k, j, *long_chain)
        elif kind == 1:
            advance(k, j, *short_chain)
        else:
            finish(j)
        if at + 1 == len(order) or order[at + 1][:2] != (slot, j):
            for work, *given in beside.pop((slot, j), []):
                work(*given)

    def put(n, low, high):
        piece[n, :quarter, :] = jnp.where(lane < part, low, turn(high))
        piece[n, quarter:, :] = jnp.where(lane < part, turn(low), high)

    for j in reversed(SENT):
        for other in (0, 1):
            x_arrival(j, other).wait_recv()
        put(block_row(-OWNED[j]), x_recv[j - 1, 0], x_recv[j - 1, 1])
    y_copy.wait_recv()
    which = jnp.full(lane.shape, my_half, jnp.int32)
    put(
        block_row(nb // 2),
        jnp.where(which == 0, y_own[...], y_recv[...]),
        jnp.where(which == 0, y_recv[...], y_own[...]),
    )

    across = (trees // 8, 4, 2)
    steps = [(a, b, c) for a in range(across[0]) for b in range(4) for c in range(2)][1:]

    def hops(step):
        return sum(min(d, n - d) for d, n in zip(step[:2], across[:2]))

    steps.sort(key=hops, reverse=True)

    def moved(step, sign):
        y, x, core = f // 8, f // 2 % 4, f % 2
        y = (y + sign * step[0] + across[0]) % across[0]
        x = (x + sign * step[1] + 4) % 4
        return y * 8 + x * 2 + (core + step[2]) % 2

    for r, step in enumerate(steps):
        owner = moved(step, 1)
        t_send[owner] = piece[choice[owner]]
        t_copy(r, owner, f).start()

    def added(source, tile, totals):
        weight = w_recv[source]
        return tuple(totals[a] + weight[a : a + 1, :] * tile for a in range(ANC_DEV))

    zero = jnp.zeros(piece.shape[1:], jnp.float32)
    totals = added(f, piece[choice[f]], (zero,) * ANC_DEV)

    @pl.loop(1, trees)
    def _(r):
        source = (f + trees - r) % trees
        w_copy(r, source, source).wait_recv()

    for r, step in enumerate(steps):
        source = moved(step, -1)
        t_copy(r, source, source).wait_recv()
        totals = added(source, t_recv[source], totals)
    for a in range(ANC_DEV):
        out_ref[a] = totals[a]

    for j in range(len(OWNED)):
        for k in range(half):
            chain(k, j, *long_chain).wait_send()
        for k in range(half - 1):
            chain(k, j, *short_chain).wait_send()
    y_copy.wait_send()
    for j in SENT:
        for other in (0, 1):
            x_copy(j, other).wait_send()

    @pl.loop(1, trees)
    def _(r):
        w_copy(r, (f + r) % trees, f).wait_send()

    for r, step in enumerate(steps):
        t_copy(r, moved(step, 1), f).wait_send()


def solution(mesh):
    subs, trees = mesh.shape["subtree"], mesh.shape["forest"]

    def per_device(panels, pattern, child_map, ancestor_map):
        rows, depth = panels.shape[2:]
        nb = child_map.shape[2]
        block = rows // nb
        part = block // 2
        half = subs // 2
        owned = len(OWNED)
        dma = pltpu.SemaphoreType.DMA
        smem = pl.BlockSpec(memory_space=pltpu.SMEM)
        vmem = pl.BlockSpec(memory_space=pltpu.VMEM)
        f32 = jnp.float32
        out = pl.pallas_call(
            lambda *refs: kernel(subs, trees, *refs),
            name="assemble",
            out_shape=pltpu.VMEM((ANC_DEV, part, block), f32),
            in_specs=[smem, smem, smem, pl.BlockSpec(memory_space=pl.ANY)],
            out_specs=vmem,
            scratch_shapes=[
                pltpu.VMEM((nb, block, depth), jnp.bfloat16),
                pltpu.VMEM((rows + 2 * block, depth), jnp.bfloat16),
                pltpu.VMEM((nb, rows, block), f32),
                pltpu.VMEM((half, part * owned - part // 2, block), f32),
                pltpu.VMEM((half - 1, part * owned - part // 2, block), f32),
                pltpu.VMEM((nb + 1, part, block), f32),
                pltpu.VMEM((len(SENT), 2, part // 2, block), f32),
                pltpu.VMEM((len(SENT), 2, part // 2, block), f32),
                pltpu.VMEM((trees, 8, block), f32),
                pltpu.VMEM((trees, 8, block), f32),
                pltpu.VMEM((trees, part, block), f32),
                pltpu.VMEM((trees, part, block), f32),
                dma((half, owned)), dma((half, owned)),
                dma((half - 1, owned)), dma((half - 1, owned)),
                dma((len(SENT), 2)), dma((len(SENT), 2)),
                dma((trees,)), dma((trees,)),
                dma((trees,)), dma((trees,)),
                dma(()),
                pltpu.SMEM((trees,), jnp.int32),
                pltpu.VMEM((part // 2, block), f32),
                pltpu.VMEM((part // 2, block), f32),
                pltpu.VMEM((part // 2, block), f32),
                pltpu.VMEM((part // 2, block), f32),
                pltpu.VMEM((part // 2, block), f32),
                dma(()), dma(()),
            ],
            compiler_params=pltpu.CompilerParams(
                collective_id=0, has_side_effects=True, vmem_limit_bytes=60 * 2**20
            ),
        )(child_map[0, 0], pattern[0, 0], ancestor_map[0, 0], panels.reshape(nb, block, depth))
        return out[None]

    return jax.shard_map(
        per_device,
        mesh=mesh,
        in_specs=(
            P("subtree", "forest", None, None),
            P("subtree", "forest", None, None),
            P("subtree", "forest", None),
            P("subtree", "forest", None),
        ),
        out_specs=P("subtree", "forest", None, None),
        check_vma=False,
    )
```
